128 devices in a mesh: grp: 4 (over x), mem: 32 (over z, y, core).
Axes of the slice: x: 4, y: 4, z: 4, core: 2. Of those that a mesh axis runs over, the one named last changes fastest.
Arguments:
- embeddings: bfloat16 [16384, 1024], P(('grp', 'mem')), may hold values from -6 to 6
- cluster: int32 [16384, 1], P(('grp', 'mem')), may hold values from 0 to 3; in each aligned block of 128 rows (0 to 127, 128 to 255, ...) at most 64 rows name the same one
- rank: int32 [16384], P(('grp', 'mem')), may hold values from 0 to 1048575
Outputs:
- similarity: float32 [16384], P(('grp', 'mem'))
The draws below stay inside these ranges and needn't reach their ends.
Inputs may be any that keep to these rules, and one draw needn't show every extreme that they name: `cluster`: in each aligned block of 128 rows (the rows of one device) no group is named by more than 64 rows. A smaller rank is earlier; equal ranks are not earlier.
All inputs are finite; a program needn't handle non-finite values.
Results may differ from the reference program's by a relative error of at most 0.0013.
Values may be sent and summed in bfloat16 or wider, within the bound.
A program may use at most 64 MiB of HBM per device.

```python
import math
import jax
import jax.numpy as jnp
import numpy as np
from jax import lax

D = 1024
ROWS_DEV = 128
CAP = 64
POINTS = 16384
N_GRP = 4
N_MEM = 32


def place_ends(array, key, smallest, top_value):
    index_at = [jax.random.randint(jax.random.fold_in(key, axis), (), 0, length) for axis, length in enumerate(array.shape)]
    widest = array.shape.index(max(array.shape))
    beside = index_at[:widest] + [(index_at[widest] + 1) % array.shape[widest]] + index_at[widest + 1:]
    return array.at[tuple(index_at)].set(smallest).at[tuple(beside)].set(top_value)


def steps_of(own_key, extent, cuts, least, top_value):
    level, own = 1.0, jax.random.fold_in(own_key, 6)
    for position, shards_of in cuts:
        draws = jnp.exp(jax.random.uniform(jax.random.fold_in(own, position), (shards_of,), jnp.float32, least / len(cuts), top_value / len(cuts)))
        level = level * jnp.repeat(draws, extent[position] // shards_of).reshape([-1 if axis == position else 1 for axis in range(len(extent))])
    return level


def deal_out(rng, own, number, rows, amount, top, limit, skew):
    order = jax.random.permutation(rng, amount)
    heavy_load, ordinary = shares(amount, rows * top, limit, skew, True), shares(amount, rows * top, limit, skew, False)
    places = jnp.arange(amount)

    def named(sizes, offset_by):
        used = int((sizes > 0).sum())
        fixed = max(1, used // 4)
        moved = fixed + (places - fixed + offset_by * (used - fixed)) % max(1, amount - fixed)
        return jnp.zeros((amount,), jnp.int32).at[order[jnp.where(places < fixed, places, moved)]].set(jnp.asarray(sizes, jnp.int32))

    sizes = jnp.where(number % 4 == 0, named(heavy_load, number // 4), named(ordinary, number - number // 4 - 1))
    mixed = jax.random.permutation(jax.random.fold_in(own, 3), amount)
    giver, taker = mixed[0:amount // 2 * 2:2], mixed[1:amount // 2 * 2:2]
    room = jnp.minimum(sizes[giver] - 1, limit - sizes[taker]) // 2
    room = jnp.where((giver == order[0]) | (taker == order[0]) | (sizes[taker] == 0), 0, jnp.maximum(room, 0))
    moved = jax.random.randint(jax.random.fold_in(own, 4), (amount // 2,), 0, 1 << 20) % (room + 1)
    sizes = sizes.at[giver].add(-moved).at[taker].add(moved)
    labels = jnp.searchsorted(jnp.cumsum(sizes), jnp.arange(rows * top), side="right").astype(jnp.int32)
    listing = labels.reshape(top, rows).T
    listing = listing[jax.random.permutation(jax.random.fold_in(own, 1), rows)]
    offset_by = jax.random.randint(jax.random.fold_in(own, 2), (rows, 1), 0, top)
    return jnp.take_along_axis(listing, (jnp.arange(top)[None, :] + offset_by) % top, axis=1)


def shares(amount, total, reach, lean, full):
    portions = [(1 << 20) // math.isqrt(grade ** lean) + 1 for grade in range(1, amount + 1)]
    largest = reach if full else min(reach, max(-(-total // amount), total * portions[0] // sum(portions)))
    least = 1 if total - largest >= amount - 1 else 0
    counts, spare = [largest] + [least] * (amount - 1), total - largest - least * (amount - 1)
    while spare > 0:
        candidates = [i for i in range(1, amount) if counts[i] < largest] or [i for i in range(1, amount) if counts[i] < reach]
        mass, left = sum([portions[i] for i in candidates]), spare
        for i in candidates:
            addition = min(reach - counts[i], max(1, left * portions[i] // mass), spare)
            counts[i] = counts[i] + addition
            spare = spare - addition
    return np.array(counts)


def noise(rng, dims, width, most, cuts=(), kind=jnp.bfloat16):
    gain = steps_of(rng, dims, cuts, -0.22, 0.18) if cuts else 1.0
    drawn = jax.random.normal(rng, dims, jnp.float32) * width * gain
    return jnp.minimum(jnp.maximum(drawn, -most), most).astype(kind)


def setup_inputs(seed: int = 0) -> dict:
    keys = jax.random.split(jax.random.key(seed), 4)
    embeddings = noise(keys[0], (POINTS, D), 1.0, 6.0, ((0, 128),))
    cluster_keys = jax.random.split(jax.random.fold_in(keys[1], 1), POINTS // ROWS_DEV)
    cluster_turns = jax.random.permutation(jax.random.fold_in(keys[1], 3), POINTS // ROWS_DEV)
    cluster = jax.vmap(lambda own, number: deal_out(jax.random.fold_in(keys[1], 2), own, number, ROWS_DEV, N_GRP, 1, CAP, 2))(cluster_keys, cluster_turns).reshape((POINTS, 1))
    rank = place_ends(jax.random.randint(keys[2], (POINTS,), 0, 1048576), jax.random.fold_in(keys[2], 1), 0, 1048575).astype(jnp.int32)
    return {"embeddings": embeddings, "cluster": cluster, "rank": rank}


def reference(embeddings, cluster, rank):
    wide = embeddings.astype(jnp.float32)
    normed = (wide * lax.rsqrt(lax.optimization_barrier(jnp.sum(wide * wide, axis=1, keepdims=True)) + 1e-06)).astype(jnp.bfloat16)
    owner = cluster[:, 0].astype(jnp.int32)
    sort_key = owner * 2097152 + rank
    order = jnp.argsort(sort_key, stable=True).astype(jnp.int32)
    span = N_GRP * N_MEM * CAP
    block = math.gcd(POINTS, 512)
    sorted_keys = jnp.concatenate([jnp.zeros((span, D), jnp.bfloat16), normed[order]], axis=0)
    sorted_owner = jnp.concatenate([jnp.full((span,), -1, jnp.int32), owner[order]], axis=0)
    sorted_rank = jnp.concatenate([jnp.zeros((span,), jnp.int32), rank[order]], axis=0)

    def one_block(index):
        start = (index * block).astype(jnp.int32)
        queries = lax.dynamic_slice_in_dim(sorted_keys, start + span, block, 0)
        query_owner = lax.dynamic_slice_in_dim(sorted_owner, start + span, block, 0)
        query_rank = lax.dynamic_slice_in_dim(sorted_rank, start + span, block, 0)
        window = lax.dynamic_slice_in_dim(sorted_keys, start, span + block, 0)
        window_owner = lax.dynamic_slice_in_dim(sorted_owner, start, span + block, 0)
        window_rank = lax.dynamic_slice_in_dim(sorted_rank, start, span + block, 0)
        gram = jnp.dot(queries, window.T, preferred_element_type=jnp.float32)
        earlier = (window_owner[None, :] == query_owner[:, None]) & (window_rank[None, :] < query_rank[:, None])
        return lax.optimization_barrier(jnp.max(jnp.where(earlier, gram, jnp.float32(-1.0)), axis=1))
    values = lax.map(one_block, jnp.arange(POINTS // block, dtype=jnp.int32)).reshape(POINTS)
    return jnp.zeros((POINTS,), jnp.float32).at[order].set(values)
```

```python
import jax
import jax.numpy as jnp
from jax import lax
from jax.experimental import pallas as pl
from jax.experimental.pallas import tpu as pltpu
from jax.sharding import PartitionSpec as P

MESH = pl.DeviceIdType.MESH
OFFSETS = (
    (0, 0, 0), (0, 0, 1), (0, 0, 2), (0, 0, 3), (0, 1, 0), (0, 2, 0), (1, 0, 0),
    (1, 1, 0), (1, 2, 0), (1, 3, 0), (3, 0, 0), (3, 0, 1), (3, 0, 2),
)
UNITS = ((1, 0, 0), (3, 0, 0), (0, 1, 0), (0, 3, 0), (0, 0, 1), (0, 0, 3))
PIECES = 4
PROGRAM = (
    ("s", 1, 2, 0, 4), ("s", 3, 0, 0, 5), ("s", 4, 0, 0, 2), ("s", 6, 1, 0, 0), ("s", 10, 0, 0, 1),
    ("x", 0), ("s", 1, 3, 0, 4), ("s", 3, 1, 0, 5), ("s", 4, 2, 0, 2), ("s", 6, 3, 0, 0),
    ("s", 10, 1, 0, 1), ("u", 0, 0), ("s", 1, 0, 0, 4), ("s", 3, 2, 0, 5), ("s", 4, 1, 0, 2),
    ("s", 6, 0, 0, 0), ("s", 10, 2, 0, 1), ("s", 9, 1, 6, 3), ("s", 2, 0, 3, 5), ("s", 4, 3, 0, 2),
    ("s", 7, 0, 4, 0), ("s", 11, 0, 10, 4), ("s", 11, 2, 1, 1), ("s", 9, 3, 6, 3), ("s", 1, 1, 0, 4),
    ("s", 2, 1, 3, 5), ("s", 5, 2, 4, 2), ("s", 6, 2, 0, 0), ("s", 11, 3, 1, 1), ("s", 9, 0, 6, 3),
    ("s", 3, 3, 0, 5), ("s", 5, 0, 4, 2), ("s", 7, 1, 4, 0), ("s", 10, 3, 0, 1), ("s", 11, 1, 10, 4),
    ("s", 8, 1, 9, 3), ("x", 4), ("u", 4, 0), ("s", 2, 2, 3, 5), ("s", 7, 2, 4, 0),
    ("s", 8, 0, 7, 2), ("s", 12, 0, 2, 1), ("s", 12, 2, 11, 4), ("s", 9, 2, 6, 3), ("x", 1),
    ("x", 6), ("u", 1, 0), ("u", 6, 0), ("s", 5, 1, 4, 2), ("s", 8, 2, 5, 0),
    ("s", 12, 1, 2, 1), ("s", 12, 3, 11, 4), ("u", 1, 4), ("u", 6, 4), ("s", 2, 3, 3, 5),
    ("s", 8, 3, 9, 3), ("x", 3), ("x", 10), ("x", 11), ("u", 3, 4),
    ("u", 10, 4), ("u", 11, 0), ("s", 5, 3, 4, 2), ("s", 7, 3, 4, 0), ("u", 11, 4),
    ("u", 3, 1), ("u", 3, 6), ("u", 10, 6), ("u", 11, 6), ("x", 9),
    ("u", 9, 1), ("u", 9, 4), ("u", 3, 11), ("x", 12), ("u", 9, 3),
    ("u", 9, 10), ("x", 2), ("u", 9, 11), ("u", 12, 4), ("u", 12, 6),
    ("u", 2, 4), ("u", 8, 1), ("u", 8, 3), ("u", 8, 6), ("u", 8, 10),
    ("u", 8, 11), ("u", 2, 9), ("u", 12, 9), ("u", 5, 1), ("u", 7, 3),
    ("u", 7, 11), ("u", 5, 12), ("u", 8, 12), ("u", 5, 2),
)
HALF = 128
WIDTH = 1024
RANKS = 1048576


def schedule():
    steps = list(PROGRAM)
    last = {}
    shared = sorted({s[1] for s in steps if s[0] == "x"})
    for i, step in enumerate(steps):
        if step[0] == "u":
            last[("own", step[1])] = i
            for which in ("own", "other"):
                last[(which, step[2])] = i
    return steps, shared, last


def kernel(
    x_hbm, cluster_ref, rank_ref, out_ref, raw, blocks, keys, key_columns, row_best, column_best,
    results, returned, raw_sem, send, receive, key_send, key_receive, pair_send, pair_receive,
    pair_key_send, pair_key_receive, back_send, back_receive,
):
    x = lax.axis_index("grp")
    m = lax.axis_index("mem")
    z, y, core = m // 8, (m // 2) % 4, m % 2
    count = len(OFFSETS)
    rows = HALF // PIECES

    def at(offset, which):
        dx, dy, dz = offset
        chip = ((z + dz) % 4) * 8 + ((y + dy) % 4) * 2
        return ((x + dx) % 4, chip + which)

    barrier = pltpu.get_barrier_semaphore()
    for unit in UNITS:
        pl.semaphore_signal(barrier, inc=1, device_id=at(unit, core), device_id_type=MESH)
    pl.semaphore_signal(
        barrier, inc=1, device_id=at((0, 0, 0), 1 - core), device_id_type=MESH
    )
    load = pltpu.make_async_copy(x_hbm, raw, raw_sem)
    load.start()
    keys[0, core] = cluster_ref[...] * (2 * RANKS) + rank_ref[...]
    row_best[...] = jnp.full(row_best.shape, -1.0, jnp.float32)
    column_best[...] = jnp.full(column_best.shape, -1.0, jnp.float32)
    load.wait()
    wide = raw[...].astype(jnp.float32)
    scale = lax.rsqrt(jnp.sum(wide * wide, axis=1, keepdims=True) + 1e-06)
    blocks[0, core] = (wide * scale).astype(jnp.bfloat16)
    pl.semaphore_wait(barrier, 7)

    steps, shared, last = schedule()
    sent = []
    arrived = set((0, piece) for piece in range(PIECES))
    key_here = {0}
    pair_here = set()
    columns_here = set()

    def copy(source, target, send_sem, receive_sem, device):
        return pltpu.make_async_remote_copy(
            src_ref=source, dst_ref=target, send_sem=send_sem, recv_sem=receive_sem,
            device_id=device, device_id_type=MESH,
        )

    def piece_copy(slot, piece, parent, direction):
        back = UNITS[direction ^ 1]
        part = pl.ds(piece * rows, rows)
        return copy(
            blocks.at[parent, core, part], blocks.at[slot, core, part],
            send.at[slot, piece], receive.at[slot, piece], at(back, core),
        )

    def key_copy(slot, parent, direction):
        back = UNITS[direction ^ 1]
        return copy(
            keys.at[parent, core], keys.at[slot, core],
            key_send.at[slot], key_receive.at[slot], at(back, core),
        )

    def pair_copy(slot):
        return copy(
            blocks.at[slot, core], blocks.at[slot, core],
            pair_send.at[slot], pair_receive.at[slot], at((0, 0, 0), 1 - core),
        )

    def pair_key_copy(slot):
        return copy(
            keys.at[slot, core], keys.at[slot, core],
            pair_key_send.at[slot], pair_key_receive.at[slot], at((0, 0, 0), 1 - core),
        )

    incoming = {(s[1], s[2]): s[1:] for s in steps if s[0] == "s"}

    def need_piece(slot, piece):
        if (slot, piece) not in arrived:
            piece_copy(*incoming[(slot, piece)]).wait_recv()
            arrived.add((slot, piece))

    def need_key(slot):
        if slot not in key_here:
            _, _, parent, direction = incoming[(slot, 0)]
            key_copy(slot, parent, direction).wait_recv()
            key_here.add(slot)

    def need_block(slot):
        for piece in range(PIECES):
            need_piece(slot, piece)
        need_key(slot)

    def need_pair(slot):
        if slot not in pair_here:
            copy(
                blocks.at[slot, 1 - core], blocks.at[slot, 1 - core],
                pair_send.at[slot], pair_receive.at[slot], at((0, 0, 0), 1 - core),
            ).wait_recv()
            copy(
                keys.at[slot, 1 - core], keys.at[slot, 1 - core],
                pair_key_send.at[slot], pair_key_receive.at[slot], at((0, 0, 0), 1 - core),
            ).wait_recv()
            pair_here.add(slot)

    def need_columns(slot):
        if slot not in columns_here:
            key_columns[slot] = jnp.broadcast_to(keys[slot, core], (HALF, HALF)).T
            columns_here.add(slot)

    def multiply(a, b):
        need_block(a)
        need_block(b)
        need_pair(b)
        need_columns(a)
        gram = lax.dot_general(
            blocks[a, core], blocks[b].reshape(2 * HALF, WIDTH), (((1,), (1,)), ((), ())),
            preferred_element_type=jnp.float32,
        )
        best = row_best[a]
        for half in range(2):
            part = gram[:, half * HALF : (half + 1) * HALF]
            gap = key_columns[a] - keys[b, half]
            part = jnp.where(jnp.abs(gap) < RANKS, part, -1.0)
            best = jnp.maximum(best, jnp.where(gap > 0, part, -1.0))
            lower = jnp.where(gap < 0, part, -1.0).reshape(HALF // 8, 8, HALF)
            column_best[b, half] = jnp.maximum(column_best[b, half], jnp.max(lower, axis=0))
        row_best[a] = best

    ready = []

    def back_copy(which, slot):
        place = slot if which == "own" else count + slot
        device = at(OFFSETS[slot], core if which == "own" else 1 - core)
        return copy(
            results.at[place], returned.at[place],
            back_send.at[place], back_receive.at[place], device,
        )

    def finish(which, slot):
        place = slot if which == "own" else count + slot
        if which == "own":
            value = jnp.max(row_best[slot].T, axis=0, keepdims=True)
            if slot in shared:
                value = jnp.maximum(
                    value, jnp.max(column_best[slot, core], axis=0, keepdims=True)
                )
        else:
            value = jnp.max(column_best[slot, 1 - core], axis=0, keepdims=True)
        results[place] = value

    def send_back():
        for which, slot in ready:
            if (which, slot) != ("own", 0):
                c = back_copy(which, slot)
                c.start()
                sent.append(c)
        ready.clear()

    for i, step in enumerate(steps):
        if step[0] == "s":
            _, slot, piece, parent, direction = step
            need_piece(parent, piece)
            c = piece_copy(slot, piece, parent, direction)
            c.start()
            sent.append(c)
            if piece == 0:
                need_key(parent)
                c = key_copy(slot, parent, direction)
                c.start()
                sent.append(c)
        elif step[0] == "x":
            need_block(step[1])
            for c in (pair_copy(step[1]), pair_key_copy(step[1])):
                c.start()
                sent.append(c)
        else:
            multiply(step[1], step[2])
            send_back()
            for which, slot in sorted(k for k, v in last.items() if v == i):
                finish(which, slot)
                ready.append((which, slot))
    send_back()

    total = results[0]
    for which, slot in last:
        if (which, slot) != ("own", 0):
            back_copy(which, slot).wait_recv()
            place = slot if which == "own" else count + slot
            total = jnp.maximum(total, returned[place])
    out_ref[...] = total
    for c in sent:
        c.wait_send()


def body(embeddings, cluster, rank):
    count = len(OFFSETS)
    dma = pltpu.SemaphoreType.DMA
    vmem = pl.BlockSpec(memory_space=pltpu.VMEM)
    found = pl.pallas_call(
        kernel,
        out_shape=jax.ShapeDtypeStruct((1, HALF), jnp.float32),
        in_specs=[pl.BlockSpec(memory_space=pl.ANY), vmem, vmem],
        out_specs=vmem,
        scratch_shapes=[
            pltpu.VMEM((HALF, WIDTH), jnp.bfloat16),
            pltpu.VMEM((count, 2, HALF, WIDTH), jnp.bfloat16),
            pltpu.VMEM((count, 2, 1, HALF), jnp.int32),
            pltpu.VMEM((count, HALF, HALF), jnp.int32),
            pltpu.VMEM((count, HALF, HALF), jnp.float32),
            pltpu.VMEM((count, 2, 8, HALF), jnp.float32),
            pltpu.VMEM((2 * count, 1, HALF), jnp.float32),
            pltpu.VMEM((2 * count, 1, HALF), jnp.float32),
            dma(()),
            dma((count, PIECES)),
            dma((count, PIECES)),
            dma((count,)),
            dma((count,)),
            dma((count,)),
            dma((count,)),
            dma((count,)),
            dma((count,)),
            dma((2 * count,)),
            dma((2 * count,)),
        ],
        compiler_params=pltpu.CompilerParams(collective_id=0, has_side_effects=True),
        name="pairs",
    )(embeddings, cluster.reshape(1, HALF), rank.reshape(1, HALF))
    return found.reshape(HALF)


def solution(mesh):
    in_specs = (P(("grp", "mem"), None), P(("grp", "mem"), None), P(("grp", "mem")))
    out_specs = P(("grp", "mem"))
    return jax.shard_map(body, mesh=mesh, in_specs=in_specs, out_specs=out_specs, check_vma=False)
```

```python
import jax
import jax.numpy as jnp
from jax import lax
from jax.experimental import pallas as pl
from jax.experimental.pallas import tpu as pltpu
from jax.sharding import PartitionSpec as P

MESH = pl.DeviceIdType.MESH
OFFSETS = (
    (0, 0, 0), (0, 0, 1), (0, 0, 2), (0, 0, 3), (0, 1, 0), (0, 3, 0), (0, 3, 1),
    (0, 3, 2), (1, 1, 0), (2, 0, 0), (2, 1, 0), (3, 0, 0), (3, 1, 0),
)
UNITS = ((1, 0, 0), (3, 0, 0), (0, 1, 0), (0, 3, 0), (0, 0, 1), (0, 0, 3))
PIECES = 4
PROGRAM = (
    ("s", 11, 3, 0, 1), ("s", 4, 1, 0, 2), ("s", 5, 0, 0, 3), ("s", 1, 1, 0, 4), ("s", 3, 2, 0, 5),
    ("x", 0), ("s", 11, 2, 0, 1), ("s", 4, 2, 0, 2), ("s", 5, 1, 0, 3), ("s", 1, 0, 0, 4),
    ("s", 3, 3, 0, 5), ("s", 11, 1, 0, 1), ("s", 4, 0, 0, 2), ("s", 5, 2, 0, 3), ("s", 1, 3, 0, 4),
    ("s", 3, 0, 0, 5), ("s", 8, 1, 4, 0), ("s", 11, 0, 0, 1), ("s", 12, 3, 11, 2), ("s", 6, 1, 1, 3),
    ("s", 1, 2, 0, 4), ("s", 2, 2, 3, 5), ("s", 8, 2, 4, 0), ("s", 9, 3, 11, 1), ("s", 12, 2, 11, 2),
    ("s", 5, 3, 0, 3), ("s", 6, 0, 5, 4), ("s", 2, 3, 3, 5), ("s", 8, 0, 4, 0), ("s", 12, 1, 4, 1),
    ("s", 4, 3, 0, 2), ("s", 6, 3, 1, 3), ("s", 6, 2, 5, 4), ("s", 3, 1, 0, 5), ("s", 10, 1, 8, 0),
    ("x", 1), ("x", 11), ("s", 9, 0, 11, 1), ("s", 12, 0, 11, 2), ("s", 7, 2, 2, 3),
    ("s", 7, 1, 6, 4), ("s", 2, 0, 3, 5), ("x", 5), ("s", 10, 0, 8, 0), ("u", 1, 0, 1, 5),
    ("s", 10, 2, 12, 1), ("s", 10, 3, 9, 2), ("s", 7, 3, 2, 3), ("s", 7, 0, 6, 4), ("u", 11, 0, 1, 5),
    ("s", 2, 1, 3, 5), ("x", 3), ("x", 4), ("x", 6), ("u", 1, 6, 3, 4),
    ("u", 11, 4), ("s", 8, 3, 4, 0), ("s", 9, 1, 11, 1), ("u", 5, 4), ("x", 12),
    ("u", 1, 12), ("u", 5, 12), ("u", 6, 3, 4, 12), ("s", 9, 2, 11, 1), ("u", 3, 12, 11),
    ("x", 10), ("u", 4, 7, 10), ("u", 11, 7), ("u", 0, 10), ("x", 2),
    ("u", 1, 10), ("u", 3, 10), ("u", 5, 10), ("u", 6, 10, 8), ("u", 12, 7),
    ("u", 10, 2, 7), ("u", 11, 2), ("u", 1, 8, 9), ("u", 3, 8), ("u", 2, 8, 9),
)
HALF = 128
WIDTH = 1024
RANKS = 1048576


def schedule():
    steps = list(PROGRAM)
    last = {}
    shared = sorted({s[1] for s in steps if s[0] == "x"})
    for i, step in enumerate(steps):
        if step[0] == "u":
            for a in step[2:]:
                last[("own", a)] = i
            for which in ("own", "other"):
                last[(which, step[1])] = i
    return steps, shared, last


def kernel(
    x_hbm, cluster_ref, rank_ref, out_ref, raw, blocks, keys, key_columns, row_best, column_best,
    results, returned, raw_sem, send, receive, key_send, key_receive, pair_send, pair_receive,
    pair_key_send, pair_key_receive, back_send, back_receive,
):
    x = lax.axis_index("grp")
    m = lax.axis_index("mem")
    z, y, core = m // 8, (m // 2) % 4, m % 2
    count = len(OFFSETS)
    rows = HALF // PIECES

    def at(offset, which):
        dx, dy, dz = offset
        chip = ((z + dz) % 4) * 8 + ((y + dy) % 4) * 2
        return ((x + dx) % 4, chip + which)

    barrier = pltpu.get_barrier_semaphore()
    for unit in UNITS:
        pl.semaphore_signal(barrier, inc=1, device_id=at(unit, core), device_id_type=MESH)
    pl.semaphore_signal(
        barrier, inc=1, device_id=at((0, 0, 0), 1 - core), device_id_type=MESH
    )
    load = pltpu.make_async_copy(x_hbm, raw, raw_sem)
    load.start()
    keys[0, core] = cluster_ref[...] * (2 * RANKS) + rank_ref[...]
    row_best[...] = jnp.full(row_best.shape, -1.0, jnp.float32)
    column_best[...] = jnp.full(column_best.shape, -1.0, jnp.float32)
    load.wait()
    wide = raw[...].astype(jnp.float32)
    scale = lax.rsqrt(jnp.sum(wide * wide, axis=1, keepdims=True) + 1e-06)
    blocks[0, core] = (wide * scale).astype(jnp.bfloat16)
    pl.semaphore_wait(barrier, 7)

    steps, shared, last = schedule()
    back_place = {k: i for i, k in enumerate(k for k in sorted(last) if k != ("own", 0))}
    arrived = set((0, piece) for piece in range(PIECES))
    key_here = {0}
    pair_here = set()
    columns_here = set()

    def copy(source, target, send_sem, receive_sem, device):
        return pltpu.make_async_remote_copy(
            src_ref=source, dst_ref=target, send_sem=send_sem, recv_sem=receive_sem,
            device_id=device, device_id_type=MESH,
        )

    def piece_copy(slot, piece, parent, direction):
        back = UNITS[direction ^ 1]
        part = pl.ds(piece * rows, rows)
        return copy(
            blocks.at[parent, core, part], blocks.at[slot, core, part],
            send, receive.at[slot, piece], at(back, core),
        )

    def key_copy(slot, parent, direction):
        back = UNITS[direction ^ 1]
        return copy(
            keys.at[parent, core], keys.at[slot, core],
            key_send, key_receive.at[slot], at(back, core),
        )

    def pair_copy(slot):
        return copy(
            blocks.at[slot, core], blocks.at[slot, core],
            pair_send, pair_receive.at[slot], at((0, 0, 0), 1 - core),
        )

    def pair_key_copy(slot):
        return copy(
            keys.at[slot, core], keys.at[slot, core],
            pair_key_send, pair_key_receive.at[slot], at((0, 0, 0), 1 - core),
        )

    incoming = {(s[1], s[2]): s[1:] for s in steps if s[0] == "s"}

    def need_piece(slot, piece):
        if (slot, piece) not in arrived:
            piece_copy(*incoming[(slot, piece)]).wait_recv()
            arrived.add((slot, piece))

    def need_key(slot):
        if slot not in key_here:
            _, _, parent, direction = incoming[(slot, 0)]
            key_copy(slot, parent, direction).wait_recv()
            key_here.add(slot)

    def need_block(slot):
        for piece in range(PIECES):
            need_piece(slot, piece)
        need_key(slot)

    def need_pair(slot):
        if slot not in pair_here:
            copy(
                blocks.at[slot, 1 - core], blocks.at[slot, 1 - core],
                pair_send, pair_receive.at[slot], at((0, 0, 0), 1 - core),
            ).wait_recv()
            copy(
                keys.at[slot, 1 - core], keys.at[slot, 1 - core],
                pair_key_send, pair_key_receive.at[slot], at((0, 0, 0), 1 - core),
            ).wait_recv()
            pair_here.add(slot)

    def need_columns(slot):
        if slot not in columns_here:
            key_columns[slot] = jnp.broadcast_to(keys[slot, core], (HALF, HALF)).T
            columns_here.add(slot)

    def multiply(b, others):
        for a in others:
            need_block(a)
        need_block(b)
        need_pair(b)
        for a in others:
            need_columns(a)
        gram = lax.dot_general(
            jnp.concatenate([blocks[a, core] for a in others], axis=0),
            blocks[b].reshape(2 * HALF, WIDTH), (((1,), (1,)), ((), ())),
            preferred_element_type=jnp.float32,
        )
        for i, a in enumerate(others):
            best = row_best[a]
            for half in range(2):
                part = gram[i * HALF : (i + 1) * HALF, half * HALF : (half + 1) * HALF]
                gap = key_columns[a] - keys[b, half]
                part = jnp.where(jnp.abs(gap) < RANKS, part, -1.0)
                best = jnp.maximum(best, jnp.where(gap > 0, part, -1.0))
                lower = jnp.where(gap < 0, part, -1.0).reshape(HALF // 8, 8, HALF)
                column_best[b, half] = jnp.maximum(column_best[b, half], jnp.max(lower, axis=0))
            row_best[a] = best

    ready = []

    def back_copy(which, slot):
        place = back_place[(which, slot)]
        device = at(OFFSETS[slot], core if which == "own" else 1 - core)
        return copy(
            results.at[place], returned.at[place],
            back_send, back_receive, device,
        )

    def finish(which, slot):
        if which == "own":
            value = jnp.max(row_best[slot].T, axis=0, keepdims=True)
            if slot in shared:
                value = jnp.maximum(
                    value, jnp.max(column_best[slot, core], axis=0, keepdims=True)
                )
        else:
            value = jnp.max(column_best[slot, 1 - core], axis=0, keepdims=True)
        results[back_place.get((which, slot), len(back_place))] = value

    def send_back():
        for which, slot in ready:
            if (which, slot) != ("own", 0):
                c = back_copy(which, slot)
                c.start()
        ready.clear()

    for i, step in enumerate(steps):
        if step[0] == "s":
            _, slot, piece, parent, direction = step
            need_piece(parent, piece)
            c = piece_copy(slot, piece, parent, direction)
            c.start()
            if piece == 0:
                need_key(parent)
                c = key_copy(slot, parent, direction)
                c.start()
        elif step[0] == "x":
            need_block(step[1])
            for c in (pair_copy(step[1]), pair_key_copy(step[1])):
                c.start()
        else:
            multiply(step[1], step[2:])
            send_back()
            for which, slot in sorted(k for k, v in last.items() if v == i):
                finish(which, slot)
                ready.append((which, slot))
    send_back()

    arrays = len(back_place)
    back = copy(
        results.at[pl.ds(0, arrays)], returned.at[pl.ds(0, arrays)],
        back_send, back_receive, at((0, 0, 0), 1 - core),
    )
    back.wait_recv()
    total = jnp.maximum(results[arrays], jnp.max(returned[pl.ds(0, arrays)], axis=0))
    out_ref[...] = total
    back.wait_send()
    passed, pairs = pl.ds(0, count - 1), pl.ds(0, len(shared))
    partner = at((0, 0, 0), 1 - core)
    copy(blocks.at[passed, core], blocks.at[passed, core], send, receive.at[0, 0], partner).wait_send()
    copy(keys.at[passed, core], keys.at[passed, core], key_send, receive.at[0, 0], partner).wait_send()
    copy(blocks.at[pairs, core], blocks.at[pairs, core], pair_send, receive.at[0, 0], partner).wait_send()
    copy(keys.at[pairs, core], keys.at[pairs, core], pair_key_send, receive.at[0, 0], partner).wait_send()


def body(embeddings, cluster, rank):
    count = len(OFFSETS)
    dma = pltpu.SemaphoreType.DMA
    vmem = pl.BlockSpec(memory_space=pltpu.VMEM)
    found = pl.pallas_call(
        kernel,
        out_shape=jax.ShapeDtypeStruct((1, HALF), jnp.float32),
        in_specs=[pl.BlockSpec(memory_space=pl.ANY), vmem, vmem],
        out_specs=vmem,
        scratch_shapes=[
            pltpu.VMEM((HALF, WIDTH), jnp.bfloat16),
            pltpu.VMEM((count, 2, HALF, WIDTH), jnp.bfloat16),
            pltpu.VMEM((count, 2, 1, HALF), jnp.int32),
            pltpu.VMEM((count, HALF, HALF), jnp.int32),
            pltpu.VMEM((count, HALF, HALF), jnp.float32),
            pltpu.VMEM((count, 2, 8, HALF), jnp.float32),
            pltpu.VMEM((2 * count, 1, HALF), jnp.float32),
            pltpu.VMEM((2 * count, 1, HALF), jnp.float32),
            dma(()),
            dma(()),
            dma((count, PIECES)),
            dma(()),
            dma((count,)),
            dma(()),
            dma((count,)),
            dma(()),
            dma((count,)),
            dma(()),
            dma(()),
        ],
        compiler_params=pltpu.CompilerParams(collective_id=0, has_side_effects=True),
        name="pairs",
    )(embeddings, cluster.reshape(1, HALF), rank.reshape(1, HALF))
    return found.reshape(HALF)


def solution(mesh):
    in_specs = (P(("grp", "mem"), None), P(("grp", "mem"), None), P(("grp", "mem")))
    out_specs = P(("grp", "mem"))
    return jax.shard_map(body, mesh=mesh, in_specs=in_specs, out_specs=out_specs, check_vma=False)
```

```python
import jax
import jax.numpy as jnp
from jax import lax
from jax.experimental import pallas as pl
from jax.experimental.pallas import tpu as pltpu
from jax.sharding import PartitionSpec as P

MESH = pl.DeviceIdType.MESH
OFFSETS = (
    (0, 0, 0), (0, 0, 1), (0, 0, 3), (0, 1, 0), (0, 1, 1), (0, 2, 0), (0, 2, 1),
    (0, 3, 0), (1, 0, 0), (1, 0, 3), (2, 0, 0), (2, 0, 3), (3, 0, 3),
)
UNITS = ((1, 0, 0), (3, 0, 0), (0, 1, 0), (0, 3, 0), (0, 0, 1), (0, 0, 3))
PIECES = 4
PROGRAM = (
    ("s", 1, 2, 0, 4), ("s", 2, 1, 0, 5), ("s", 3, 0, 0, 2), ("s", 7, 0, 0, 3), ("s", 8, 1, 0, 0),
    ("s", 1, 3, 0, 4), ("s", 2, 3, 0, 5), ("s", 3, 1, 0, 2), ("s", 7, 1, 0, 3), ("s", 8, 2, 0, 0),
    ("s", 1, 1, 0, 4), ("s", 2, 0, 0, 5), ("s", 3, 2, 0, 2), ("s", 7, 3, 0, 3), ("s", 8, 0, 0, 0),
    ("s", 2, 2, 0, 5), ("s", 8, 3, 0, 0), ("s", 12, 1, 2, 1), ("s", 4, 0, 3, 4), ("s", 4, 2, 1, 2),
    ("s", 5, 0, 7, 3), ("s", 9, 1, 8, 5), ("s", 12, 3, 2, 1), ("s", 4, 1, 3, 4), ("s", 4, 3, 1, 2),
    ("s", 5, 1, 7, 3), ("s", 10, 2, 8, 0), ("s", 1, 0, 0, 4), ("s", 9, 2, 8, 5), ("s", 12, 0, 2, 1),
    ("s", 5, 2, 3, 2), ("s", 5, 3, 7, 3), ("s", 10, 0, 8, 0), ("s", 7, 2, 0, 3), ("s", 12, 2, 2, 1),
    ("s", 6, 0, 5, 4), ("s", 6, 2, 4, 2), ("s", 9, 3, 8, 5), ("s", 10, 3, 8, 0), ("s", 9, 0, 8, 5),
    ("s", 10, 1, 8, 0), ("x", 2), ("x", 8), ("s", 11, 3, 12, 1), ("s", 11, 1, 12, 1),
    ("s", 6, 1, 5, 4), ("s", 6, 3, 4, 2), ("s", 3, 3, 0, 2), ("x", 4), ("u", 8, 4, 0, 2, 8),
    ("s", 11, 0, 10, 5), ("s", 11, 2, 9, 0), ("x", 1), ("x", 5), ("u", 8, 5, 1),
    ("u", 2, 1), ("u", 4, 0, 1, 2, 5), ("x", 12), ("u", 4, 12), ("x", 7),
    ("u", 4, 7), ("x", 6), ("u", 2, 6), ("u", 8, 6, 9), ("u", 4, 9, 10),
    ("u", 5, 10), ("u", 12, 6, 1, 5, 8, 9), ("u", 7, 9, 10, 12, 8), ("u", 1, 11), ("u", 4, 11),
    ("u", 5, 11), ("u", 7, 11, 3), ("u", 12, 3), ("u", 8, 3), ("u", 6, 11),
)
HALF = 128
WIDTH = 1024
RANKS = 1048576


def schedule():
    steps = list(PROGRAM)
    last = {}
    shared = sorted({s[1] for s in steps if s[0] == "x"})
    for i, step in enumerate(steps):
        if step[0] == "u":
            for a in step[2:]:
                last[("own", a)] = i
            for which in ("own", "other"):
                last[(which, step[1])] = i
    return steps, shared, last


def kernel(
    x_hbm, cluster_ref, rank_ref, out_ref, raw, blocks, keys, key_columns, row_best, column_best,
    results, returned, raw_sem, send, receive, key_send, key_receive, pair_send, pair_receive,
    pair_key_send, pair_key_receive, back_send, back_receive,
):
    x = lax.axis_index("grp")
    m = lax.axis_index("mem")
    z, y, core = m // 8, (m // 2) % 4, m % 2
    count = len(OFFSETS)
    rows = HALF // PIECES

    def at(offset, which):
        dx, dy, dz = offset
        chip = ((z + dz) % 4) * 8 + ((y + dy) % 4) * 2
        return ((x + dx) % 4, chip + which)

    barrier = pltpu.get_barrier_semaphore()
    for unit in UNITS:
        pl.semaphore_signal(barrier, inc=1, device_id=at(unit, core), device_id_type=MESH)
    pl.semaphore_signal(
        barrier, inc=1, device_id=at((0, 0, 0), 1 - core), device_id_type=MESH
    )
    load = pltpu.make_async_copy(x_hbm, raw, raw_sem)
    load.start()
    keys[0, core] = cluster_ref[...] * (2 * RANKS) + rank_ref[...]
    row_best[...] = jnp.full(row_best.shape, -1.0, jnp.float32)
    column_best[...] = jnp.full(column_best.shape, -1.0, jnp.float32)
    load.wait()
    wide = raw[...].astype(jnp.float32)
    scale = lax.rsqrt(jnp.sum(wide * wide, axis=1, keepdims=True) + 1e-06)
    blocks[0, core] = (wide * scale).astype(jnp.bfloat16)
    pl.semaphore_wait(barrier, 7)

    steps, shared, last = schedule()
    back_place = {k: i for i, k in enumerate(k for k in sorted(last) if k != ("own", 0))}
    arrived = set((0, piece) for piece in range(PIECES))
    key_here = {0}
    pair_here = set()
    columns_here = set()

    def copy(source, target, send_sem, receive_sem, device):
        return pltpu.make_async_remote_copy(
            src_ref=source, dst_ref=target, send_sem=send_sem, recv_sem=receive_sem,
            device_id=device, device_id_type=MESH,
        )

    def piece_copy(slot, piece, parent, direction):
        back = UNITS[direction ^ 1]
        part = pl.ds(piece * rows, rows)
        return copy(
            blocks.at[parent, core, part], blocks.at[slot, core, part],
            send, receive.at[slot, piece], at(back, core),
        )

    def key_copy(slot, parent, direction):
        back = UNITS[direction ^ 1]
        return copy(
            keys.at[parent, core], keys.at[slot, core],
            key_send, key_receive.at[slot], at(back, core),
        )

    def pair_copy(slot):
        return copy(
            blocks.at[slot, core], blocks.at[slot, core],
            pair_send, pair_receive.at[slot], at((0, 0, 0), 1 - core),
        )

    def pair_key_copy(slot):
        return copy(
            keys.at[slot, core], keys.at[slot, core],
            pair_key_send, pair_key_receive.at[slot], at((0, 0, 0), 1 - core),
        )

    incoming = {(s[1], s[2]): s[1:] for s in steps if s[0] == "s"}

    def need_piece(slot, piece):
        if (slot, piece) not in arrived:
            piece_copy(*incoming[(slot, piece)]).wait_recv()
            arrived.add((slot, piece))

    def need_key(slot):
        if slot not in key_here:
            _, _, parent, direction = incoming[(slot, 0)]
            key_copy(slot, parent, direction).wait_recv()
            key_here.add(slot)

    def need_block(slot):
        for piece in range(PIECES):
            need_piece(slot, piece)
        need_key(slot)

    def need_pair(slot):
        if slot not in pair_here:
            copy(
                blocks.at[slot, 1 - core], blocks.at[slot, 1 - core],
                pair_send, pair_receive.at[slot], at((0, 0, 0), 1 - core),
            ).wait_recv()
            copy(
                keys.at[slot, 1 - core], keys.at[slot, 1 - core],
                pair_key_send, pair_key_receive.at[slot], at((0, 0, 0), 1 - core),
            ).wait_recv()
            pair_here.add(slot)

    def need_columns(slot):
        if slot not in columns_here:
            key_columns[slot] = jnp.broadcast_to(keys[slot, core], (HALF, HALF)).T
            columns_here.add(slot)

    def need(b, others):
        for a in others:
            need_block(a)
        need_block(b)
        need_pair(b)
        for a in others:
            need_columns(a)

    def multiply(b, others):
        gram = lax.dot_general(
            jnp.concatenate([blocks[a, core] for a in others], axis=0),
            blocks[b].reshape(2 * HALF, WIDTH), (((1,), (1,)), ((), ())),
            preferred_element_type=jnp.float32,
        )
        for i, a in enumerate(others):
            best = row_best[a]
            for half in range(2):
                part = gram[i * HALF : (i + 1) * HALF, half * HALF : (half + 1) * HALF]
                gap = key_columns[a] - keys[b, half]
                part = jnp.where(jnp.abs(gap) < RANKS, part, -1.0)
                best = jnp.maximum(best, jnp.where(gap > 0, part, -1.0))
                lower = jnp.where(gap < 0, part, -1.0).reshape(HALF // 8, 8, HALF)
                column_best[b, half] = jnp.maximum(column_best[b, half], jnp.max(lower, axis=0))
            row_best[a] = best

    ready = []

    def back_copy(which, slot):
        place = back_place[(which, slot)]
        device = at(OFFSETS[slot], core if which == "own" else 1 - core)
        return copy(
            results.at[place], returned.at[place],
            back_send, back_receive, device,
        )

    def finish(which, slot):
        if which == "own":
            value = jnp.max(row_best[slot].T, axis=0, keepdims=True)
            if slot in shared:
                value = jnp.maximum(
                    value, jnp.max(column_best[slot, core], axis=0, keepdims=True)
                )
        else:
            value = jnp.max(column_best[slot, 1 - core], axis=0, keepdims=True)
        results[back_place.get((which, slot), len(back_place))] = value

    def send_back():
        for which, slot in ready:
            if (which, slot) != ("own", 0):
                c = back_copy(which, slot)
                c.start()
        ready.clear()

    i = 0
    while i < len(steps):
        step = steps[i]
        if step[0] == "u":
            batch = []
            while i < len(steps) and steps[i][0] == "u":
                batch.append(steps[i])
                i += 1
            for unit in batch:
                need(unit[1], unit[2:])
            for unit in batch:
                multiply(unit[1], unit[2:])
            send_back()
            for key in sorted(k for k, v in last.items() if i - len(batch) <= v < i):
                finish(*key)
                ready.append(key)
            continue
        if step[0] == "s":
            _, slot, piece, parent, direction = step
            need_piece(parent, piece)
            piece_copy(slot, piece, parent, direction).start()
            if piece == 0:
                need_key(parent)
                key_copy(slot, parent, direction).start()
        else:
            need_block(step[1])
            pair_copy(step[1]).start()
            pair_key_copy(step[1]).start()
        send_back()
        i += 1
    send_back()

    arrays = len(back_place)
    back = copy(
        results.at[pl.ds(0, arrays)], returned.at[pl.ds(0, arrays)],
        back_send, back_receive, at((0, 0, 0), 1 - core),
    )
    back.wait_recv()
    total = jnp.maximum(results[arrays], jnp.max(returned[pl.ds(0, arrays)], axis=0))
    out_ref[...] = total
    back.wait_send()
    passed, pairs = pl.ds(0, count - 1), pl.ds(0, len(shared))
    partner = at((0, 0, 0), 1 - core)
    copy(blocks.at[passed, core], blocks.at[passed, core], send, receive.at[0, 0], partner).wait_send()
    copy(keys.at[passed, core], keys.at[passed, core], key_send, receive.at[0, 0], partner).wait_send()
    copy(blocks.at[pairs, core], blocks.at[pairs, core], pair_send, receive.at[0, 0], partner).wait_send()
    copy(keys.at[pairs, core], keys.at[pairs, core], pair_key_send, receive.at[0, 0], partner).wait_send()


def body(embeddings, cluster, rank):
    count = len(OFFSETS)
    dma = pltpu.SemaphoreType.DMA
    vmem = pl.BlockSpec(memory_space=pltpu.VMEM)
    found = pl.pallas_call(
        kernel,
        out_shape=jax.ShapeDtypeStruct((1, HALF), jnp.float32),
        in_specs=[pl.BlockSpec(memory_space=pl.ANY), vmem, vmem],
        out_specs=vmem,
        scratch_shapes=[
            pltpu.VMEM((HALF, WIDTH), jnp.bfloat16),
            pltpu.VMEM((count, 2, HALF, WIDTH), jnp.bfloat16),
            pltpu.VMEM((count, 2, 1, HALF), jnp.int32),
            pltpu.VMEM((count, HALF, HALF), jnp.int32),
            pltpu.VMEM((count, HALF, HALF), jnp.float32),
            pltpu.VMEM((count, 2, 8, HALF), jnp.float32),
            pltpu.VMEM((2 * count, 1, HALF), jnp.float32),
            pltpu.VMEM((2 * count, 1, HALF), jnp.float32),
            dma(()),
            dma(()),
            dma((count, PIECES)),
            dma(()),
            dma((count,)),
            dma(()),
            dma((count,)),
            dma(()),
            dma((count,)),
            dma(()),
            dma(()),
        ],
        compiler_params=pltpu.CompilerParams(collective_id=0, has_side_effects=True),
        name="pairs",
    )(embeddings, cluster.reshape(1, HALF), rank.reshape(1, HALF))
    return found.reshape(HALF)


def solution(mesh):
    in_specs = (P(("grp", "mem"), None), P(("grp", "mem"), None), P(("grp", "mem")))
    out_specs = P(("grp", "mem"))
    return jax.shard_map(body, mesh=mesh, in_specs=in_specs, out_specs=out_specs, check_vma=False)
```

```python
import jax
import jax.numpy as jnp
from jax import lax
from jax.experimental import pallas as pl
from jax.experimental.pallas import tpu as pltpu
from jax.sharding import PartitionSpec as P

MESH = pl.DeviceIdType.MESH
OFFSETS = (
    (0, 0, 0), (0, 0, 1), (0, 0, 3), (0, 1, 0), (0, 1, 1), (0, 2, 0), (0, 2, 1),
    (0, 3, 0), (1, 0, 0), (1, 0, 3), (2, 0, 0), (2, 0, 3), (3, 0, 3),
)
UNITS = ((1, 0, 0), (3, 0, 0), (0, 1, 0), (0, 3, 0), (0, 0, 1), (0, 0, 3))
PIECES = 4
PROGRAM = (
    ("s", 1, 2, 0, 4), ("s", 2, 1, 0, 5), ("s", 3, 0, 0, 2), ("s", 7, 0, 0, 3), ("s", 8, 1, 0, 0),
    ("s", 1, 3, 0, 4), ("s", 2, 3, 0, 5), ("s", 3, 1, 0, 2), ("s", 7, 1, 0, 3), ("s", 8, 2, 0, 0),
    ("s", 1, 1, 0, 4), ("s", 2, 0, 0, 5), ("s", 3, 2, 0, 2), ("s", 7, 3, 0, 3), ("s", 8, 0, 0, 0),
    ("s", 2, 2, 0, 5), ("s", 8, 3, 0, 0), ("s", 12, 1, 2, 1), ("s", 4, 0, 3, 4), ("s", 4, 2, 1, 2),
    ("s", 5, 0, 7, 3), ("s", 9, 1, 8, 5), ("s", 12, 3, 2, 1), ("s", 4, 1, 3, 4), ("s", 4, 3, 1, 2),
    ("s", 5, 1, 7, 3), ("s", 10, 2, 8, 0), ("s", 1, 0, 0, 4), ("s", 9, 2, 8, 5), ("s", 12, 0, 2, 1),
    ("s", 5, 2, 3, 2), ("s", 5, 3, 7, 3), ("s", 10, 0, 8, 0), ("s", 7, 2, 0, 3), ("s", 12, 2, 2, 1),
    ("s", 6, 0, 5, 4), ("s", 6, 2, 4, 2), ("s", 9, 3, 8, 5), ("s", 10, 3, 8, 0), ("s", 9, 0, 8, 5),
    ("s", 10, 1, 8, 0), ("x", 2), ("x", 8), ("s", 11, 3, 12, 1), ("s", 11, 1, 12, 1),
    ("s", 6, 1, 5, 4), ("s", 6, 3, 4, 2), ("s", 3, 3, 0, 2), ("x", 4), ("u", 8, 4, 0, 2, 8),
    ("s", 11, 0, 10, 5), ("s", 11, 2, 9, 0), ("x", 1), ("x", 5), ("u", 8, 5, 1),
    ("u", 2, 1), ("u", 4, 0, 1, 2, 5), ("x", 12), ("u", 4, 12), ("x", 7),
    ("u", 4, 7), ("x", 6), ("u", 2, 6), ("u", 8, 6, 9), ("u", 4, 9, 10),
    ("u", 5, 10), ("u", 12, 6, 1, 5, 8, 9), ("u", 7, 9, 10, 12, 8), ("u", 1, 11), ("u", 4, 11),
    ("u", 5, 11), ("u", 7, 11, 3), ("u", 12, 3), ("u", 8, 3), ("u", 6, 11),
)
HALF = 128
WIDTH = 1024
RANKS = 1048576


def schedule():
    steps = list(PROGRAM)
    last = {}
    shared = sorted({s[1] for s in steps if s[0] == "x"})
    for i, step in enumerate(steps):
        if step[0] == "u":
            for a in step[2:]:
                last[("own", a)] = i
            for which in ("own", "other"):
                last[(which, step[1])] = i
    return steps, shared, last


def kernel(
    x_hbm, cluster_hbm, rank_hbm, out_ref, raw, labels, label_sem, blocks, keys, key_columns, row_best, column_best,
    results, returned, raw_sem, send, receive, key_send, key_receive, pair_send, pair_receive,
    pair_key_send, pair_key_receive, back_send, back_receive,
):
    x = lax.axis_index("grp")
    m = lax.axis_index("mem")
    z, y, core = m // 8, (m // 2) % 4, m % 2
    count = len(OFFSETS)
    rows = HALF // PIECES

    def at(offset, which):
        dx, dy, dz = offset
        chip = ((z + dz) % 4) * 8 + ((y + dy) % 4) * 2
        return ((x + dx) % 4, chip + which)

    barrier = pltpu.get_barrier_semaphore()
    for unit in UNITS:
        pl.semaphore_signal(barrier, inc=1, device_id=at(unit, core), device_id_type=MESH)
    pl.semaphore_signal(
        barrier, inc=1, device_id=at((0, 0, 0), 1 - core), device_id_type=MESH
    )
    load = pltpu.make_async_copy(x_hbm, raw, raw_sem)
    load.start()
    label_loads = [
        pltpu.make_async_copy(source, labels.at[i], label_sem.at[i])
        for i, source in enumerate((cluster_hbm, rank_hbm))
    ]
    for c in label_loads:
        c.start()
    row_best[...] = jnp.full(row_best.shape, -1.0, jnp.float32)
    column_best[...] = jnp.full(column_best.shape, -1.0, jnp.float32)
    for c in label_loads:
        c.wait()
    keys[0, core] = labels[0] * (2 * RANKS) + labels[1]
    load.wait()
    wide = raw[...].astype(jnp.float32)
    scale = lax.rsqrt(jnp.sum(wide * wide, axis=1, keepdims=True) + 1e-06)
    blocks[0, core] = (wide * scale).astype(jnp.bfloat16)
    pl.semaphore_wait(barrier, 7)

    steps, shared, last = schedule()
    back_place = {k: i for i, k in enumerate(k for k in sorted(last) if k != ("own", 0))}
    arrived = set((0, piece) for piece in range(PIECES))
    key_here = {0}
    pair_here = set()
    columns_here = set()

    def copy(source, target, send_sem, receive_sem, device):
        return pltpu.make_async_remote_copy(
            src_ref=source, dst_ref=target, send_sem=send_sem, recv_sem=receive_sem,
            device_id=device, device_id_type=MESH,
        )

    def piece_copy(slot, piece, parent, direction):
        back = UNITS[direction ^ 1]
        part = pl.ds(piece * rows, rows)
        return copy(
            blocks.at[parent, core, part], blocks.at[slot, core, part],
            send, receive.at[slot - 1, piece], at(back, core),
        )

    def key_copy(slot, parent, direction):
        back = UNITS[direction ^ 1]
        return copy(
            keys.at[parent, core], keys.at[slot, core],
            key_send, key_receive.at[slot - 1], at(back, core),
        )

    def pair_copy(slot):
        return copy(
            blocks.at[slot, core], blocks.at[slot, core],
            pair_send, pair_receive.at[shared.index(slot)], at((0, 0, 0), 1 - core),
        )

    def pair_key_copy(slot):
        return copy(
            keys.at[slot, core], keys.at[slot, core],
            pair_key_send, pair_key_receive.at[shared.index(slot)], at((0, 0, 0), 1 - core),
        )

    incoming = {(s[1], s[2]): s[1:] for s in steps if s[0] == "s"}

    def need_piece(slot, piece):
        if (slot, piece) not in arrived:
            piece_copy(*incoming[(slot, piece)]).wait_recv()
            arrived.add((slot, piece))

    def need_key(slot):
        if slot not in key_here:
            _, _, parent, direction = incoming[(slot, 0)]
            key_copy(slot, parent, direction).wait_recv()
            key_here.add(slot)

    def need_block(slot):
        for piece in range(PIECES):
            need_piece(slot, piece)
        need_key(slot)

    def need_pair(slot):
        if slot not in pair_here:
            copy(
                blocks.at[slot, 1 - core], blocks.at[slot, 1 - core],
                pair_send, pair_receive.at[shared.index(slot)], at((0, 0, 0), 1 - core),
            ).wait_recv()
            copy(
                keys.at[slot, 1 - core], keys.at[slot, 1 - core],
                pair_key_send, pair_key_receive.at[shared.index(slot)], at((0, 0, 0), 1 - core),
            ).wait_recv()
            pair_here.add(slot)

    def need_columns(slot):
        if slot not in columns_here:
            key_columns[slot] = jnp.broadcast_to(keys[slot, core], (HALF, HALF)).T
            columns_here.add(slot)

    def need(b, others):
        for a in others:
            need_block(a)
        need_block(b)
        need_pair(b)
        for a in others:
            need_columns(a)

    def multiply(b, others):
        gram = lax.dot_general(
            jnp.concatenate([blocks[a, core] for a in others], axis=0),
            blocks[b].reshape(2 * HALF, WIDTH), (((1,), (1,)), ((), ())),
            preferred_element_type=jnp.float32,
        )
        for i, a in enumerate(others):
            best = row_best[a]
            for half in range(2):
                part = gram[i * HALF : (i + 1) * HALF, half * HALF : (half + 1) * HALF]
                gap = key_columns[a] - keys[b, half]
                part = jnp.where(jnp.abs(gap) < RANKS, part, -1.0)
                best = jnp.maximum(best, jnp.where(gap > 0, part, -1.0))
                lower = jnp.where(gap < 0, part, -1.0).reshape(HALF // 8, 8, HALF)
                column_best[b, half] = jnp.maximum(column_best[b, half], jnp.max(lower, axis=0))
            row_best[a] = best

    ready = []

    def back_copy(which, slot):
        place = back_place[(which, slot)]
        device = at(OFFSETS[slot], core if which == "own" else 1 - core)
        return copy(
            results.at[place], returned.at[place],
            back_send, back_receive, device,
        )

    def finish(which, slot):
        if which == "own":
            value = jnp.max(row_best[slot].T, axis=0, keepdims=True)
            if slot in shared:
                value = jnp.maximum(
                    value, jnp.max(column_best[slot, core], axis=0, keepdims=True)
                )
        else:
            value = jnp.max(column_best[slot, 1 - core], axis=0, keepdims=True)
        results[back_place.get((which, slot), len(back_place))] = value

    def send_back():
        for which, slot in ready:
            if (which, slot) != ("own", 0):
                c = back_copy(which, slot)
                c.start()
        ready.clear()

    i = 0
    while i < len(steps):
        step = steps[i]
        if step[0] == "u":
            batch = []
            while i < len(steps) and steps[i][0] == "u":
                batch.append(steps[i])
                i += 1
            for unit in batch:
                need(unit[1], unit[2:])
            for unit in batch:
                multiply(unit[1], unit[2:])
            send_back()
            for key in sorted(k for k, v in last.items() if i - len(batch) <= v < i):
                finish(*key)
                ready.append(key)
            continue
        if step[0] == "s":
            _, slot, piece, parent, direction = step
            need_piece(parent, piece)
            piece_copy(slot, piece, parent, direction).start()
            if piece == 0:
                need_key(parent)
                key_copy(slot, parent, direction).start()
        else:
            need_block(step[1])
            pair_copy(step[1]).start()
            pair_key_copy(step[1]).start()
        send_back()
        i += 1
    send_back()

    arrays = len(back_place)
    back = copy(
        results.at[pl.ds(0, arrays)], returned.at[pl.ds(0, arrays)],
        back_send, back_receive, at((0, 0, 0), 1 - core),
    )
    back.wait_recv()
    total = jnp.maximum(results[arrays], jnp.max(returned[pl.ds(0, arrays)], axis=0))
    out_ref[...] = total
    back.wait_send()
    passed, pairs = pl.ds(0, count - 1), pl.ds(0, len(shared))
    partner = at((0, 0, 0), 1 - core)
    copy(blocks.at[passed, core], blocks.at[passed, core], send, receive.at[0, 0], partner).wait_send()
    copy(keys.at[passed, core], keys.at[passed, core], key_send, receive.at[0, 0], partner).wait_send()
    copy(blocks.at[pairs, core], blocks.at[pairs, core], pair_send, receive.at[0, 0], partner).wait_send()
    copy(keys.at[pairs, core], keys.at[pairs, core], pair_key_send, receive.at[0, 0], partner).wait_send()


def body(embeddings, cluster, rank):
    count, shared = len(OFFSETS), len(schedule()[1])
    dma = pltpu.SemaphoreType.DMA
    vmem = pl.BlockSpec(memory_space=pltpu.VMEM)
    found = pl.pallas_call(
        kernel,
        out_shape=jax.ShapeDtypeStruct((1, HALF), jnp.float32),
        in_specs=[pl.BlockSpec(memory_space=pl.ANY)] * 3,
        out_specs=vmem,
        scratch_shapes=[
            pltpu.VMEM((HALF, WIDTH), jnp.bfloat16),
            pltpu.VMEM((2, 1, HALF), jnp.int32),
            dma((2,)),
            pltpu.VMEM((count, 2, HALF, WIDTH), jnp.bfloat16),
            pltpu.VMEM((count, 2, 1, HALF), jnp.int32),
            pltpu.VMEM((count, HALF, HALF), jnp.int32),
            pltpu.VMEM((count, HALF, HALF), jnp.float32),
            pltpu.VMEM((count, 2, 8, HALF), jnp.float32),
            pltpu.VMEM((2 * count, 1, HALF), jnp.float32),
            pltpu.VMEM((2 * count, 1, HALF), jnp.float32),
            dma(()),
            dma(()),
            dma((count - 1, PIECES)),
            dma(()),
            dma((count - 1,)),
            dma(()),
            dma((shared,)),
            dma(()),
            dma((shared,)),
            dma(()),
            dma(()),
        ],
        compiler_params=pltpu.CompilerParams(collective_id=0, has_side_effects=True),
        name="pairs",
    )(embeddings, cluster.reshape(1, HALF), rank.reshape(1, HALF))
    return found.reshape(HALF)


def solution(mesh):
    in_specs = (P(("grp", "mem"), None), P(("grp", "mem"), None), P(("grp", "mem")))
    out_specs = P(("grp", "mem"))
    return jax.shard_map(body, mesh=mesh, in_specs=in_specs, out_specs=out_specs, check_vma=False)
```

```python
import jax
import jax.numpy as jnp
from jax import lax
from jax.experimental import pallas as pl
from jax.experimental.pallas import tpu as pltpu
from jax.sharding import PartitionSpec as P

MESH = pl.DeviceIdType.MESH
OFFSETS = (
    (0, 0, 0), (0, 0, 1), (0, 0, 3), (0, 1, 0), (0, 1, 1), (0, 2, 0), (0, 2, 1),
    (0, 3, 0), (1, 0, 0), (1, 0, 3), (2, 0, 0), (2, 0, 3), (3, 0, 3),
)
UNITS = ((1, 0, 0), (3, 0, 0), (0, 1, 0), (0, 3, 0), (0, 0, 1), (0, 0, 3))
PIECES = 4
PROGRAM = (
    ("s", 1, 2, 0, 4), ("s", 2, 1, 0, 5), ("s", 3, 0, 0, 2), ("s", 7, 0, 0, 3), ("s", 8, 1, 0, 0),
    ("s", 1, 3, 0, 4), ("s", 2, 3, 0, 5), ("s", 3, 1, 0, 2), ("s", 7, 1, 0, 3), ("s", 8, 2, 0, 0),
    ("s", 1, 1, 0, 4), ("s", 2, 0, 0, 5), ("s", 3, 2, 0, 2), ("s", 7, 3, 0, 3), ("s", 8, 0, 0, 0),
    ("s", 2, 2, 0, 5), ("s", 8, 3, 0, 0), ("s", 12, 1, 2, 1), ("s", 4, 0, 3, 4), ("s", 4, 2, 1, 2),
    ("s", 5, 0, 7, 3), ("s", 9, 1, 8, 5), ("s", 12, 3, 2, 1), ("s", 4, 1, 3, 4), ("s", 4, 3, 1, 2),
    ("s", 5, 1, 7, 3), ("s", 10, 2, 8, 0), ("s", 1, 0, 0, 4), ("s", 9, 2, 8, 5), ("s", 12, 0, 2, 1),
    ("s", 5, 2, 3, 2), ("s", 5, 3, 7, 3), ("s", 10, 0, 8, 0), ("s", 7, 2, 0, 3), ("s", 12, 2, 2, 1),
    ("s", 6, 0, 5, 4), ("s", 6, 2, 4, 2), ("s", 9, 3, 8, 5), ("s", 10, 3, 8, 0), ("s", 9, 0, 8, 5),
    ("s", 10, 1, 8, 0), ("x", 2), ("x", 8), ("s", 11, 3, 12, 1), ("s", 11, 1, 12, 1),
    ("s", 6, 1, 5, 4), ("s", 6, 3, 4, 2), ("s", 3, 3, 0, 2), ("x", 4), ("u", 8, 4, 0, 2, 8),
    ("s", 11, 0, 10, 5), ("s", 11, 2, 9, 0), ("x", 1), ("x", 5), ("u", 8, 5, 1),
    ("v", 2, 1), ("v", 4, 0, 1, 2, 5), ("x", 12), ("u", 4, 12), ("x", 7),
    ("u", 4, 7), ("x", 6), ("u", 2, 6), ("v", 8, 6), ("v", 12, 6),
    ("v", 6, 11), ("v", 1, 11), ("v", 4, 11), ("v", 5, 11), ("v", 7, 11),
    ("u", 8, 9, 3), ("v", 4, 9, 10), ("v", 5, 10), ("v", 12, 1, 5, 8, 9, 3), ("v", 7, 9, 10, 12, 8, 3),
)
HALF = 128
WIDTH = 1024
RANKS = 1048576


def schedule():
    steps = list(PROGRAM)
    last = {}
    shared = sorted({s[1] for s in steps if s[0] == "x"})
    for i, step in enumerate(steps):
        if step[0] in "uv":
            for a in step[2:]:
                last[("own", a)] = i
            for which in ("own", "other"):
                last[(which, step[1])] = i
    return steps, shared, last


def kernel(
    x_hbm, cluster_hbm, rank_hbm, out_ref, raw, labels, label_sem, blocks, keys, key_columns, row_best, column_best,
    results, returned, raw_sem, send, receive, key_send, key_receive, pair_send, pair_receive,
    pair_key_send, pair_key_receive, back_send, back_receive,
):
    x = lax.axis_index("grp")
    m = lax.axis_index("mem")
    z, y, core = m // 8, (m // 2) % 4, m % 2
    count = len(OFFSETS)
    rows = HALF // PIECES

    def at(offset, which):
        dx, dy, dz = offset
        chip = ((z + dz) % 4) * 8 + ((y + dy) % 4) * 2
        return ((x + dx) % 4, chip + which)

    barrier = pltpu.get_barrier_semaphore()
    for unit in UNITS:
        pl.semaphore_signal(barrier, inc=1, device_id=at(unit, core), device_id_type=MESH)
    pl.semaphore_signal(
        barrier, inc=1, device_id=at((0, 0, 0), 1 - core), device_id_type=MESH
    )
    load = pltpu.make_async_copy(x_hbm, raw, raw_sem)
    load.start()
    label_loads = [
        pltpu.make_async_copy(source, labels.at[i], label_sem.at[i])
        for i, source in enumerate((cluster_hbm, rank_hbm))
    ]
    for c in label_loads:
        c.start()
    row_best[...] = jnp.full(row_best.shape, -1.0, jnp.float32)
    column_best[...] = jnp.full(column_best.shape, -1.0, jnp.float32)
    for c in label_loads:
        c.wait()
    keys[0, core] = labels[0] * (2 * RANKS) + labels[1]
    load.wait()
    wide = raw[...].astype(jnp.float32)
    scale = lax.rsqrt(jnp.sum(wide * wide, axis=1, keepdims=True) + 1e-06)
    blocks[0, core] = (wide * scale).astype(jnp.bfloat16)
    pl.semaphore_wait(barrier, 7)

    steps, shared, last = schedule()
    back_place = {k: i for i, k in enumerate(k for k in sorted(last) if k != ("own", 0))}
    arrived = set((0, piece) for piece in range(PIECES))
    key_here = {0}
    pair_here = set()
    columns_here = set()

    def copy(source, target, send_sem, receive_sem, device):
        return pltpu.make_async_remote_copy(
            src_ref=source, dst_ref=target, send_sem=send_sem, recv_sem=receive_sem,
            device_id=device, device_id_type=MESH,
        )

    def piece_copy(slot, piece, parent, direction):
        back = UNITS[direction ^ 1]
        part = pl.ds(piece * rows, rows)
        return copy(
            blocks.at[parent, core, part], blocks.at[slot, core, part],
            send, receive.at[slot - 1, piece], at(back, core),
        )

    def key_copy(slot, parent, direction):
        back = UNITS[direction ^ 1]
        return copy(
            keys.at[parent, core], keys.at[slot, core],
            key_send, key_receive.at[slot - 1], at(back, core),
        )

    def pair_copy(slot):
        return copy(
            blocks.at[slot, core], blocks.at[slot, core],
            pair_send, pair_receive.at[shared.index(slot)], at((0, 0, 0), 1 - core),
        )

    def pair_key_copy(slot):
        return copy(
            keys.at[slot, core], keys.at[slot, core],
            pair_key_send, pair_key_receive.at[shared.index(slot)], at((0, 0, 0), 1 - core),
        )

    incoming = {(s[1], s[2]): s[1:] for s in steps if s[0] == "s"}

    def need_piece(slot, piece):
        if (slot, piece) not in arrived:
            piece_copy(*incoming[(slot, piece)]).wait_recv()
            arrived.add((slot, piece))

    def need_key(slot):
        if slot not in key_here:
            _, _, parent, direction = incoming[(slot, 0)]
            key_copy(slot, parent, direction).wait_recv()
            key_here.add(slot)

    def need_block(slot):
        for piece in range(PIECES):
            need_piece(slot, piece)
        need_key(slot)

    def need_pair(slot):
        if slot not in pair_here:
            copy(
                blocks.at[slot, 1 - core], blocks.at[slot, 1 - core],
                pair_send, pair_receive.at[shared.index(slot)], at((0, 0, 0), 1 - core),
            ).wait_recv()
            copy(
                keys.at[slot, 1 - core], keys.at[slot, 1 - core],
                pair_key_send, pair_key_receive.at[shared.index(slot)], at((0, 0, 0), 1 - core),
            ).wait_recv()
            pair_here.add(slot)

    def need_columns(slot):
        if slot not in columns_here:
            key_columns[slot] = jnp.broadcast_to(keys[slot, core], (HALF, HALF)).T
            columns_here.add(slot)

    def need(b, others):
        for a in others:
            need_block(a)
        need_block(b)
        need_pair(b)
        for a in others:
            need_columns(a)

    def multiply(b, others):
        gram = lax.dot_general(
            jnp.concatenate([blocks[a, core] for a in others], axis=0),
            blocks[b].reshape(2 * HALF, WIDTH), (((1,), (1,)), ((), ())),
            preferred_element_type=jnp.float32,
        )
        for i, a in enumerate(others):
            best = row_best[a]
            for half in range(2):
                part = gram[i * HALF : (i + 1) * HALF, half * HALF : (half + 1) * HALF]
                gap = key_columns[a] - keys[b, half]
                part = jnp.where(jnp.abs(gap) < RANKS, part, -1.0)
                best = jnp.maximum(best, jnp.where(gap > 0, part, -1.0))
                lower = jnp.where(gap < 0, part, -1.0).reshape(HALF // 8, 8, HALF)
                column_best[b, half] = jnp.maximum(column_best[b, half], jnp.max(lower, axis=0))
            row_best[a] = best

    ready = []

    def back_copy(which, slot):
        place = back_place[(which, slot)]
        device = at(OFFSETS[slot], core if which == "own" else 1 - core)
        return copy(
            results.at[place], returned.at[place],
            back_send, back_receive, device,
        )

    def finish(which, slot):
        if which == "own":
            value = jnp.max(row_best[slot].T, axis=0, keepdims=True)
            if slot in shared:
                value = jnp.maximum(
                    value, jnp.max(column_best[slot, core], axis=0, keepdims=True)
                )
        else:
            value = jnp.max(column_best[slot, 1 - core], axis=0, keepdims=True)
        results[back_place.get((which, slot), len(back_place))] = value

    def send_back():
        for which, slot in ready:
            if (which, slot) != ("own", 0):
                c = back_copy(which, slot)
                c.start()
        ready.clear()

    i = 0
    while i < len(steps):
        step = steps[i]
        if step[0] == "u":
            batch = []
            while i < len(steps) and steps[i][0] == ("v" if batch else "u"):
                batch.append(steps[i])
                i += 1
            for unit in batch:
                need(unit[1], unit[2:])
            for unit in batch:
                multiply(unit[1], unit[2:])
            send_back()
            for key in sorted(k for k, v in last.items() if i - len(batch) <= v < i):
                finish(*key)
                ready.append(key)
            continue
        if step[0] == "s":
            _, slot, piece, parent, direction = step
            need_piece(parent, piece)
            piece_copy(slot, piece, parent, direction).start()
            if piece == 0:
                need_key(parent)
                key_copy(slot, parent, direction).start()
        else:
            need_block(step[1])
            pair_copy(step[1]).start()
            pair_key_copy(step[1]).start()
        send_back()
        i += 1
    send_back()

    arrays = len(back_place)
    back = copy(
        results.at[pl.ds(0, arrays)], returned.at[pl.ds(0, arrays)],
        back_send, back_receive, at((0, 0, 0), 1 - core),
    )
    back.wait_recv()
    total = jnp.maximum(results[arrays], jnp.max(returned[pl.ds(0, arrays)], axis=0))
    out_ref[...] = total
    back.wait_send()
    passed, pairs = pl.ds(0, count - 1), pl.ds(0, len(shared))
    partner = at((0, 0, 0), 1 - core)
    copy(blocks.at[passed, core], blocks.at[passed, core], send, receive.at[0, 0], partner).wait_send()
    copy(keys.at[passed, core], keys.at[passed, core], key_send, receive.at[0, 0], partner).wait_send()
    copy(blocks.at[pairs, core], blocks.at[pairs, core], pair_send, receive.at[0, 0], partner).wait_send()
    copy(keys.at[pairs, core], keys.at[pairs, core], pair_key_send, receive.at[0, 0], partner).wait_send()


def body(embeddings, cluster, rank):
    count, shared = len(OFFSETS), len(schedule()[1])
    dma = pltpu.SemaphoreType.DMA
    vmem = pl.BlockSpec(memory_space=pltpu.VMEM)
    found = pl.pallas_call(
        kernel,
        out_shape=jax.ShapeDtypeStruct((1, HALF), jnp.float32),
        in_specs=[pl.BlockSpec(memory_space=pl.ANY)] * 3,
        out_specs=vmem,
        scratch_shapes=[
            pltpu.VMEM((HALF, WIDTH), jnp.bfloat16),
            pltpu.VMEM((2, 1, HALF), jnp.int32),
            dma((2,)),
            pltpu.VMEM((count, 2, HALF, WIDTH), jnp.bfloat16),
            pltpu.VMEM((count, 2, 1, HALF), jnp.int32),
            pltpu.VMEM((count, HALF, HALF), jnp.int32),
            pltpu.VMEM((count, HALF, HALF), jnp.float32),
            pltpu.VMEM((count, 2, 8, HALF), jnp.float32),
            pltpu.VMEM((2 * count, 1, HALF), jnp.float32),
            pltpu.VMEM((2 * count, 1, HALF), jnp.float32),
            dma(()),
            dma(()),
            dma((count - 1, PIECES)),
            dma(()),
            dma((count - 1,)),
            dma(()),
            dma((shared,)),
            dma(()),
            dma((shared,)),
            dma(()),
            dma(()),
        ],
        compiler_params=pltpu.CompilerParams(collective_id=0, has_side_effects=True),
        name="pairs",
    )(embeddings, cluster.reshape(1, HALF), rank.reshape(1, HALF))
    return found.reshape(HALF)


def solution(mesh):
    in_specs = (P(("grp", "mem"), None), P(("grp", "mem"), None), P(("grp", "mem")))
    out_specs = P(("grp", "mem"))
    return jax.shard_map(body, mesh=mesh, in_specs=in_specs, out_specs=out_specs, check_vma=False)
```
